32 devices in a mesh: pairs: 2 (over y), pb: 4 (over z), ka: 2 (over core), wa: 2 (over x).
Axes of the slice: x: 2, y: 2, z: 4, core: 2. Of those that a mesh axis runs over, the one named last changes fastest.
Arguments:
- clean_rows: bfloat16 [4096, 8192], P(('pairs', 'pb', 'ka'), 'wa'), parts along dimension 0, may hold values from -72 to 72
- noised_rows: bfloat16 [4096, 8192], P(('pairs', 'pb', 'ka'), 'wa'), parts along dimension 0, may hold values from -6 to 6
- query_weight: bfloat16 [8192, 512], P('wa'), may hold values from -0.0625 to 0.0625
- key_weight: bfloat16 [8192, 128], P('wa'), may hold values from -0.0625 to 0.0625
- value_weight: bfloat16 [8192, 128], P('wa'), may hold values from -0.0625 to 0.0625
- out_grads: bfloat16 [4096, 512], P(('pairs', 'pb', 'ka'), 'wa'), parts along dimension 0, may hold values from -6 to 6
- lookback: int32 [4096], P('pairs'), parts along dimension 0, may hold values from 1 to 2048
Outputs:
- attribution: float32 [4096], P(('pairs', 'pb', 'ka', 'wa')), parts along dimension 0
The draws below stay inside these ranges and needn't reach their ends.
There are 2 independent parts, one for each index of `pairs`. The reference program is written for one: setup_inputs(seed, part) draws one part's arguments, and reference() takes and returns one part's arrays. A program takes and returns all parts, laid end to end along the dimension named above; an argument that names none is the same for every part. Nothing has to cross between parts.
All inputs are finite; a program needn't handle non-finite values.
Results may differ from the reference program's by a relative error of at most 0.01315.
The reference program's roundings to bfloat16 on the way (of `queries`, `keys`, `values` and `noised_keys`) count: a program that leaves them out, or rounds other values in their place, can miss the bound.
Values may be sent and summed in bfloat16 or wider, within the bound.
No kernel may reach another device: no remote copies, remote signals or barrier semaphores. Data moves between devices by JAX's collectives and lax.ppermute only.
A program may use at most 64 MiB of HBM per device.

```python
import math
import jax
import jax.numpy as jnp
from jax import lax

D = 8192
HD = 128
H = 4
TOKENS = 2048


def draw_clean_rows(key, part):
    base_key = jax.random.fold_in(jax.random.fold_in(key, 7), 0)
    rows = jax.random.truncated_normal(base_key, -6.0, 6.0, (TOKENS, D), jnp.float32)
    return rows.astype(jnp.bfloat16)


def with_ends(result, key, smallest, high):
    extent = result.shape
    place = [jax.random.randint(jax.random.fold_in(key, axis), (), 0, extent[axis]) for axis in range(len(extent))]
    result = result.at[tuple(place)].set(smallest)
    longest = extent.index(max(extent))
    place[longest] = (place[longest] + 1) % extent[longest]
    return result.at[tuple(place)].set(high)


def level_of(key, dims, cuts, least, high):
    def one(dim, shards_of):
        draws = jax.random.uniform(jax.random.fold_in(jax.random.fold_in(key, 6), dim), (shards_of,), jnp.float32, least / len(cuts), high / len(cuts))
        return jnp.repeat(jnp.exp(draws), dims[dim] // shards_of).reshape((-1,) + (1,) * (len(dims) - dim - 1))

    loudness = one(*cuts[0])
    for cut in cuts[1:]:
        loudness = loudness * one(*cut)
    return loudness


def noise(stream_key, shape, deviation, reach, cuts=(), held_as=jnp.bfloat16):
    array = deviation * jax.random.normal(stream_key, shape, jnp.float32)
    if cuts:
        array = array * level_of(stream_key, shape, cuts, -0.22, 0.18)
    return jnp.clip(array, -reach, reach).astype(held_as)


def setup_inputs(seed: int = 0, part: int = 0) -> dict:
    arg_keys = jax.random.split(jax.random.key(seed), 8)
    part_splits = jax.random.split(jax.random.fold_in(arg_keys[7], part), 8)
    clean_rows = draw_clean_rows(jax.random.fold_in(jax.random.fold_in(arg_keys[7], part), 71), part)
    noised_rows = noise(part_splits[1], (TOKENS, D), 1.0, 6.0, ((0, 8), (1, 2)))
    query_weight = noise(arg_keys[2], (D, H * HD), D ** -0.5, 0.0625, ((0, 2),))
    key_weight = noise(arg_keys[3], (D, HD), D ** -0.5, 0.0625, ((0, 2),))
    value_weight = noise(arg_keys[4], (D, HD), D ** -0.5, 0.0625, ((0, 2),))
    out_grads = noise(part_splits[5], (TOKENS, H * HD), 1.0, 6.0, ((0, 8), (1, 2)))
    lookback = with_ends(jax.random.randint(part_splits[6], (TOKENS,), 1, TOKENS + 1), jax.random.fold_in(part_splits[6], 1), 1, TOKENS).astype(jnp.int32)
    return {"clean_rows": clean_rows, "noised_rows": noised_rows, "query_weight": query_weight, "key_weight": key_weight, "value_weight": value_weight, "out_grads": out_grads, "lookback": lookback}


very_low = -1e+30

def visible_pairs(query_pos, query_look, key_pos):
    distance = query_pos[:, None] - key_pos[None, :]
    return (distance >= 0) & (distance < query_look[:, None])

def block_changes(query_block, grad_block, visible, row_parts, key_block, value_block, noised_block, score_scale):
    highest, row_total, weighted, mean_now = row_parts
    scores = jnp.einsum('bhd,kd->bhk', query_block, key_block, precision=lax.Precision.HIGHEST) * score_scale
    patched = jnp.einsum('bhd,kd->bhk', query_block, noised_block, precision=lax.Precision.HIGHEST) * score_scale
    grad_value = jnp.einsum('bhd,kd->bhk', grad_block, value_block, precision=lax.Precision.HIGHEST)
    held = highest[:, :, None]
    scores = jnp.where(visible, scores, held)
    patched = jnp.where(visible, patched, held)
    shifted = jnp.maximum(held, patched)
    factor = jnp.exp(held - shifted)
    swapped = jnp.exp(patched - shifted) - jnp.exp(scores - shifted)
    divisor = jnp.maximum(row_total[:, :, None] * factor + swapped, 1.0)
    change = (weighted[:, :, None] * factor + swapped * grad_value) / divisor - mean_now[:, :, None]
    return lax.optimization_barrier(jnp.sum(jnp.where(visible, change, 0.0), axis=(0, 1)))

def reference(clean_rows, noised_rows, query_weight, key_weight, value_weight, out_grads, lookback):
    score_scale = 1.0 / math.sqrt(HD)
    queries = jnp.dot(clean_rows, query_weight, preferred_element_type=jnp.float32).astype(jnp.bfloat16)
    keys = jnp.dot(clean_rows, key_weight, preferred_element_type=jnp.float32).astype(jnp.bfloat16)
    values = jnp.dot(clean_rows, value_weight, preferred_element_type=jnp.float32).astype(jnp.bfloat16)
    noised_keys = jnp.dot(noised_rows, key_weight, preferred_element_type=jnp.float32).astype(jnp.bfloat16)
    query_full = queries.astype(jnp.float32).reshape(TOKENS, H, HD)
    grad_full = out_grads.astype(jnp.float32).reshape(TOKENS, H, HD)
    key_full = keys.astype(jnp.float32)
    value_full = values.astype(jnp.float32)
    noised_full = noised_keys.astype(jnp.float32)
    positions = jnp.arange(TOKENS, dtype=jnp.int32)
    block_rows = min(512, TOKENS)
    attribution = jnp.zeros((TOKENS,), jnp.float32)
    for block_index in range(TOKENS // block_rows):
        first_row = block_index * block_rows
        end_row = first_row + block_rows
        query_block = query_full[first_row:end_row]
        grad_block = grad_full[first_row:end_row]
        visible = visible_pairs(positions[first_row:end_row], lookback[first_row:end_row], positions[:end_row])[:, None, :]
        scores = jnp.einsum('bhd,kd->bhk', query_block, key_full[:end_row], precision=lax.Precision.HIGHEST) * score_scale
        grad_value = jnp.einsum('bhd,kd->bhk', grad_block, value_full[:end_row], precision=lax.Precision.HIGHEST)
        masked = jnp.where(visible, scores, very_low)
        highest = lax.optimization_barrier(jnp.max(masked, axis=2))
        weights = jnp.where(visible, jnp.exp(masked - highest[:, :, None]), 0.0)
        row_total = lax.optimization_barrier(jnp.sum(weights, axis=2))
        weighted = lax.optimization_barrier(jnp.sum(weights * grad_value, axis=2))
        mean_now = weighted / row_total
        changes = block_changes(query_block, grad_block, visible, (highest, row_total, weighted, mean_now), key_full[:end_row], value_full[:end_row], noised_full[:end_row], score_scale)
        attribution = attribution.at[:end_row].add(changes)
    return attribution
```

```python
import functools
import math

import jax
import jax.numpy as jnp
from jax import lax
from jax.experimental import pallas as pl
from jax.experimental.pallas import tpu as pltpu
from jax.sharding import PartitionSpec as P

very_low = -1e30
plane_axes = ("ka", "wa")


def peer(index, step, size):
    if size & (size - 1) == 0:
        return index ^ step
    return (index + step) % size


def origin(index, step, size):
    if size & (size - 1) == 0:
        return index ^ step
    return (index - step + size) % size


def swapped_with(array, axes, step, size):
    return lax.ppermute(array, axes, [(i, peer(i, step, size)) for i in range(size)])


def pair_step(step_ka, step_wa, ka_size, wa_size):
    moves = []
    for k in range(ka_size):
        for w in range(wa_size):
            target = peer(k, step_ka, ka_size) * wa_size + peer(w, step_wa, wa_size)
            moves.append((k * wa_size + w, target))
    return moves


def dot(a, b):
    return jnp.dot(a, b, preferred_element_type=jnp.float32)


def dot_t(a, b, precision=None):
    return lax.dot_general(
        a, b, (((1,), (1,)), ((), ())), precision=precision, preferred_element_type=jnp.float32
    )


def side_kernel(wa_size, clean_ref, noised_ref, key_ref, value_ref, *rest):
    pieces, total = rest[:-1], rest[-1]
    step = pl.program_id(0)
    head = key_ref.shape[1]
    clean = clean_ref[...]
    both = dot(clean, key_ref[...]), dot(clean, value_ref[...]), dot(noised_ref[...], key_ref[...])

    @pl.when(step == 0)
    def _():
        for n, part in enumerate(both):
            total[:, n * head : (n + 1) * head] = part

    @pl.when(step > 0)
    def _():
        for n, part in enumerate(both):
            total[:, n * head : (n + 1) * head] += part

    @pl.when(step == pl.num_programs(0) - 1)
    def _():
        rows = pieces[0].shape[0]
        mine = lax.axis_index("wa")
        for n, piece in enumerate(pieces):
            start = pl.multiple_of(peer(mine, n, wa_size) * rows, rows)
            piece[...] = total[pl.ds(start, rows), :]


def side_terms(clean_rows, noised_rows, key_weight, value_weight, wa_size):
    rows, depth = clean_rows.shape
    head = key_weight.shape[1]
    chunk = math.gcd(depth, 1024)
    piece = jax.ShapeDtypeStruct((rows // wa_size, 3 * head), jnp.float32)
    wide = pl.BlockSpec((rows, chunk), lambda k: (0, k))
    tall = pl.BlockSpec((chunk, head), lambda k: (k, 0))
    return pl.pallas_call(
        functools.partial(side_kernel, wa_size),
        grid=(depth // chunk,),
        in_specs=[wide, wide, tall, tall],
        out_specs=[pl.BlockSpec(piece.shape, lambda k: (0, 0))] * wa_size,
        out_shape=[piece] * wa_size,
        scratch_shapes=[pltpu.VMEM((rows, 3 * head), jnp.float32)],
        cost_estimate=pl.CostEstimate(
            flops=6 * rows * depth * head,
            bytes_accessed=4 * rows * depth + 4 * depth * head,
            transcendentals=0,
        ),
        name="side_terms",
    )(clean_rows, noised_rows, key_weight, value_weight)


def query_kernel(clean_ref, weight_ref, out_ref):
    step = pl.program_id(0)
    part = dot(clean_ref[...], weight_ref[...])

    @pl.when(step == 0)
    def _():
        out_ref[...] = part

    @pl.when(step > 0)
    def _():
        out_ref[...] += part


def query_terms(clean_rows, query_weight):
    rows, depth = clean_rows.shape
    wide = query_weight.shape[1]
    chunk = math.gcd(depth, 1024)
    return pl.pallas_call(
        query_kernel,
        grid=(depth // chunk,),
        in_specs=[
            pl.BlockSpec((rows, chunk), lambda k: (0, k)),
            pl.BlockSpec((chunk, wide), lambda k: (k, 0)),
        ],
        out_specs=pl.BlockSpec((rows, wide), lambda k: (0, 0)),
        out_shape=jax.ShapeDtypeStruct((rows, wide), jnp.float32),
        cost_estimate=pl.CostEstimate(
            flops=2 * rows * depth * wide,
            bytes_accessed=2 * rows * depth + 2 * depth * wide,
            transcendentals=0,
        ),
        name="query_terms",
    )(clean_rows, query_weight)


class Plan:
    def __init__(self, pb, ka, wa, rows, head, heads):
        self.pb, self.ka, self.wa = pb, ka, wa
        self.rows, self.head, self.heads = rows, head, heads
        self.key_rows = rows // wa
        self.plane = ka * rows
        self.group = heads // wa
        self.factor = math.log2(math.e) / math.sqrt(head)
        self.stats = heads * self.plane


def blocks_of(plan, refs):
    query_refs, grad_refs = refs[: plan.ka], refs[plan.ka : plan.ka + plan.ka * plan.wa]
    ka_index, wa_index = lax.axis_index("ka"), lax.axis_index("wa")
    for a in range(plan.ka):
        first = pl.multiple_of(origin(ka_index, a, plan.ka) * plan.rows, plan.rows)
        for b in range(plan.wa):
            start = origin(wa_index, b, plan.wa) * plan.group
            for k in range(plan.group):
                head = start + k
                lane = pl.multiple_of(head * plan.head, plan.head)
                queries = query_refs[a][:, pl.ds(lane, plan.head)]
                grads = grad_refs[a * plan.wa + b][:, k * plan.head : (k + 1) * plan.head]
                place = pl.multiple_of(head * plan.plane + first, plan.rows)
                yield first, place, queries, grads


def visible_of(plan, step, look_ref, first):
    pb_index = lax.axis_index("pb")
    base = (pb_index - step) * plan.plane
    base += lax.axis_index("ka") * plan.rows + lax.axis_index("wa") * plan.key_rows
    look = look_ref[pl.ds(pb_index, 1), pl.ds(first, plan.rows)]
    query_pos = lax.broadcasted_iota(jnp.int32, (1, plan.rows), 1) + (
        pb_index * plan.plane + first - base
    )
    key_pos = lax.broadcasted_iota(jnp.int32, (plan.key_rows, plan.rows), 0)
    lowest = query_pos - look
    visible = key_pos > lowest
    if step == 0:
        visible &= key_pos <= query_pos
    return visible


def stats_kernel(plan, look_ref, *refs):
    count = plan.ka + plan.ka * plan.wa
    key_refs = refs[count : count + plan.pb]
    out_ref, running = refs[count + plan.pb :]
    pb_index = lax.axis_index("pb")
    size = plan.head

    def one_step(step):
        keys = key_refs[step][:, :size]
        values = key_refs[step][:, size : 2 * size]
        for first, place, queries, grads in blocks_of(plan, refs):
            visible = visible_of(plan, step, look_ref, first)
            scores = dot_t(keys, queries) * plan.factor
            grad_value = dot_t(values, grads)
            scores = jnp.where(visible, scores, very_low).reshape(-1, 8, plan.rows)
            lanes = pl.ds(place, plan.rows)
            highest = jnp.max(scores, axis=0)
            if step > 0:
                earlier = running[0, :, lanes]
                highest = jnp.maximum(earlier, highest)
            weights = jnp.exp2(scores - highest[None])
            total = jnp.sum(weights, axis=0)
            weighted = jnp.sum(weights * grad_value.reshape(weights.shape), axis=0)
            if step > 0:
                scale = jnp.exp2(earlier - highest)
                total += running[1, :, lanes] * scale
                weighted += running[2, :, lanes] * scale
            running[0, :, lanes] = highest
            running[1, :, lanes] = total
            running[2, :, lanes] = weighted

    for step in range(plan.pb):
        if step == 0:
            one_step(step)
        else:
            pl.when(pb_index >= step)(functools.partial(one_step, step))

    highest = running[0]
    top = jnp.max(highest, axis=0, keepdims=True)
    scale = jnp.exp2(highest - top)
    out_ref[:, : plan.stats] = top
    out_ref[:, plan.stats : 2 * plan.stats] = jnp.sum(running[1] * scale, axis=0, keepdims=True)
    out_ref[:, 2 * plan.stats :] = jnp.sum(running[2] * scale, axis=0, keepdims=True)


def changes_kernel(plan, look_ref, *refs):
    count = plan.ka + plan.ka * plan.wa
    key_refs = refs[count : count + plan.pb]
    stats_refs = refs[count + plan.pb : -2]
    out_ref, merged = refs[-2:]
    pb_index = lax.axis_index("pb")
    size = plan.head
    n = plan.stats

    top = functools.reduce(jnp.maximum, [ref[:, :n] for ref in stats_refs])
    scales = [jnp.exp2(ref[:, :n] - top) for ref in stats_refs]
    total = sum(ref[:, n : 2 * n] * scale for ref, scale in zip(stats_refs, scales))
    weighted = sum(ref[:, 2 * n :] * scale for ref, scale in zip(stats_refs, scales))
    merged[0:1, :] = top
    merged[1:2, :] = total
    merged[2:3, :] = weighted
    merged[3:4, :] = weighted / total
    out_ref[...] = jnp.zeros_like(out_ref)

    def one_step(step):
        keys = key_refs[step][:, :size]
        values = key_refs[step][:, size : 2 * size]
        noised = key_refs[step][:, 2 * size :]
        lane_count = min(128, plan.rows)
        summed = jnp.zeros((plan.key_rows, lane_count), jnp.float32)
        for first, place, queries, grads in blocks_of(plan, refs):
            visible = visible_of(plan, step, look_ref, first)
            scores = dot_t(keys, queries) * plan.factor
            patched = dot_t(noised, queries) * plan.factor
            grad_value = dot_t(values, grads)
            lanes = pl.ds(place, plan.rows)
            highest = merged[0:1, lanes]
            row_total = merged[1:2, lanes]
            row_weighted = merged[2:3, lanes]
            mean_now = merged[3:4, lanes]
            shifted = jnp.maximum(highest, patched)
            factor = jnp.exp2(highest - shifted)
            swapped = jnp.exp2(patched - shifted) - jnp.exp2(scores - shifted)
            divisor = jnp.maximum(row_total * factor + swapped, 1.0)
            change = (row_weighted * factor + swapped * grad_value) / divisor - mean_now
            change = jnp.where(visible, change, 0.0)
            for start in range(0, plan.rows, lane_count):
                summed += change[:, start : start + lane_count]
        ones = jnp.ones((8, lane_count), jnp.float32)
        row = dot_t(ones, summed, precision=lax.Precision.HIGHEST)
        out_ref[pl.ds(pb_index - step, 1), :] = row[0:1]

    for step in range(plan.pb):
        if step == 0:
            one_step(step)
        else:
            pl.when(pb_index >= step)(functools.partial(one_step, step))


def whole_block(array):
    return pl.BlockSpec(memory_space=pltpu.VMEM)


def stats_of(plan, look_grid, queries, grads, keys):
    operands = (look_grid, *queries, *grads, *keys)
    return pl.pallas_call(
        functools.partial(stats_kernel, plan),
        in_specs=[whole_block(x) for x in operands],
        out_specs=pl.BlockSpec(memory_space=pltpu.VMEM),
        out_shape=jax.ShapeDtypeStruct((1, 3 * plan.stats), jnp.float32),
        scratch_shapes=[pltpu.VMEM((3, 8, plan.stats), jnp.float32)],
        name="row_stats",
    )(*operands)


def changes_of(plan, look_grid, queries, grads, keys, stats):
    operands = (look_grid, *queries, *grads, *keys, *stats)
    return pl.pallas_call(
        functools.partial(changes_kernel, plan),
        in_specs=[whole_block(x) for x in operands],
        out_specs=pl.BlockSpec(memory_space=pltpu.VMEM),
        out_shape=jax.ShapeDtypeStruct((plan.pb, plan.key_rows), jnp.float32),
        scratch_shapes=[pltpu.VMEM((4, plan.stats), jnp.float32)],
        name="changes",
    )(*operands)


def shards(clean_rows, noised_rows, query_weight, key_weight, value_weight, out_grads, lookback):
    pb_size, ka_size, wa_size = (lax.axis_size(name) for name in ("pb", "ka", "wa"))
    rows = clean_rows.shape[0]
    head = key_weight.shape[1]
    plan = Plan(pb_size, ka_size, wa_size, rows, head, query_weight.shape[1] // head)
    look_grid = lookback.reshape(pb_size, plan.plane)

    pieces = side_terms(clean_rows, noised_rows, key_weight, value_weight, wa_size)
    side = pieces[0]
    for step in range(1, wa_size):
        side = side + swapped_with(pieces[step], "wa", step, wa_size)
    side = side.astype(jnp.bfloat16)

    grads = []
    for a in range(ka_size):
        for b in range(wa_size):
            if a == b == 0:
                grads.append(out_grads)
            else:
                moves = pair_step(a, b, ka_size, wa_size)
                grads.append(lax.ppermute(out_grads, plane_axes, moves))

    terms = query_terms(clean_rows, query_weight)
    summed = terms
    for step in range(1, wa_size):
        summed = summed + swapped_with(terms, "wa", step, wa_size)
    own = summed.astype(jnp.bfloat16)
    queries = [own]
    for step in range(1, ka_size):
        queries.append(swapped_with(own, "ka", step, ka_size))

    keys = [side]
    for step in range(1, pb_size):
        keys.append(lax.ppermute(side, "pb", [(i, i + step) for i in range(pb_size - step)]))

    mine = stats_of(plan, look_grid, queries, grads, keys)
    stats = [mine]
    for a in range(ka_size):
        for b in range(wa_size):
            if a or b:
                moves = pair_step(a, b, ka_size, wa_size)
                stats.append(lax.ppermute(mine, plane_axes, moves))
    part = changes_of(plan, look_grid, queries, grads, keys, stats)
    gathered = lax.all_to_all(part, "pb", 0, 0, tiled=True)
    return jnp.sum(gathered, axis=0)


def solution(mesh):
    in_specs = (
        P(("pairs", "pb", "ka"), "wa"),
        P(("pairs", "pb", "ka"), "wa"),
        P("wa", None),
        P("wa", None),
        P("wa", None),
        P(("pairs", "pb", "ka"), "wa"),
        P("pairs"),
    )
    out_specs = P(("pairs", "pb", "ka", "wa"))
    return jax.shard_map(shards, mesh=mesh, in_specs=in_specs, out_specs=out_specs, check_vma=False)
```
